32 devices in a mesh: seq: 16 (over z, y, x), tp: 2 (over core).
Axes of the slice: x: 2, y: 2, z: 4, core: 2. Of those that a mesh axis runs over, the one named last changes fastest.
Arguments:
- latent: bfloat16 [4096, 4096], P('seq', 'tp'), may hold values from -4000 to 4000
- latent_gain: bfloat16 [4096], P('tp'), may hold values from 0.099609375 to 1.8984375
- proj_weight: bfloat16 [4096, 1024], P('tp'), may hold values from -0.09375 to 0.09375
- patch_starts: int32 [4096], replicated, may hold values from 0 to 16383, as said below
- stream: bfloat16 [16384, 1024], P('seq'), may hold values from -500 to 500
- doc_starts: int32 [16384], P('seq'), may hold values from 0 to 16383, as said below
- stream_gain: bfloat16 [1024], replicated, may hold values from 0.099609375 to 1.8984375
- self_query: bfloat16 [1024, 1024], P(None, 'tp'), may hold values from -2 to 2
- self_key: bfloat16 [1024, 1024], P(None, 'tp'), may hold values from -2 to 2
- self_value: bfloat16 [1024, 1024], P(None, 'tp'), may hold values from -0.1875 to 0.1875
- self_out: bfloat16 [1024, 1024], P('tp'), may hold values from -0.1875 to 0.1875
- cross_query: bfloat16 [1024, 1024], P(None, 'tp'), may hold values from -2 to 2
- cross_key: bfloat16 [1024, 1024], P(None, 'tp'), may hold values from -2 to 2
- cross_value: bfloat16 [1024, 1024], P(None, 'tp'), may hold values from -0.1875 to 0.1875
- cross_out: bfloat16 [1024, 1024], P('tp'), may hold values from -0.1875 to 0.1875
Outputs:
- update: bfloat16 [16384, 1024], P('seq', 'tp')
The draws below stay inside these ranges and needn't reach their ends.
Inputs may be any that keep to these rules, and one draw needn't show every extreme that they name: Strictly rising with patch_starts[0] = 0. In aligned blocks of 512 bytes, the patches that start in block b are numbers c(b) to c(b + 1) - 1 with c(b) within 32 of b * 128, and a patch starts at byte b * 512 + 512 // 2 of every block. The patches that start in bytes d * 1024 - 512 to (d + 1) * 1024 - 1 number at most 448 for every d, and exactly 448 for some d. doc_starts[i] is the first byte of byte i's document: never falling, at most i, always a patch start, and equal to i exactly where a document begins.
All inputs are finite; a program needn't handle non-finite values.
Results may differ from the reference program's by a relative error of at most 0.015.
The reference program's roundings to bfloat16 on the way count: a program that leaves them out, or rounds other values in their place, can miss the bound.
Values may be sent and summed in bfloat16 or wider, within the bound.
A program may use at most 128 MiB of HBM per device.

```python
import math
import jax
import jax.numpy as jnp
from jax import lax

DL = 4096
DD = 1024
HEADS = 16
HD = 64
WIN = 512
PATCH_LEN = 4
BYTES_DEV = 1024
PATCH_DEV = 256
PMAX = 448
BYTES = 16384
PATCHES = 4096
N_SEQ = 16


def scaled_rows(key, row_count, col_count, rise):
    first_key, row_key, col_key = jax.random.split(key, 3)
    position = jnp.arange(col_count, dtype=jnp.float32) / col_count
    base_values = jnp.clip(jax.random.normal(first_key, (row_count, col_count), jnp.float32), -4.0, 4.0)
    row_scale = 10.0 ** jax.random.uniform(row_key, (row_count, 1), jnp.float32)
    col_scale = 10.0 ** jax.random.uniform(col_key, (1, col_count), jnp.float32) * rise ** position[None, :]
    return base_values * row_scale * col_scale


def layout(key):
    shift_key, rank_key, doc_key = jax.random.split(jax.random.fold_in(key, 21), 3)
    block_count = BYTES // WIN
    per_block = WIN // PATCH_LEN
    quarter = per_block // 4
    stride = BYTES_DEV // WIN
    drift = jax.random.randint(shift_key, (block_count + 1,), -quarter, quarter + 1).astype(jnp.int32)
    drift = drift.at[0].set(0).at[block_count].set(0).at[stride - 1].set(-quarter).at[2 * stride].set(quarter)
    counts = per_block + drift[1:] - drift[:-1]
    scores = jax.vmap(lambda one_key: jax.random.permutation(one_key, WIN))(jax.random.split(rank_key, block_count)).astype(jnp.int32)
    inside = jnp.arange(WIN, dtype=jnp.int32)[None, :]
    block_ids = jnp.arange(block_count, dtype=jnp.int32)[:, None]
    forced = (inside == WIN // 2) | (block_ids == 0) & (inside == 0)
    scores = jnp.where(forced, -1, scores)
    order = jnp.argsort(scores, axis=1, stable=True)
    ranks = jnp.argsort(order, axis=1, stable=True).astype(jnp.int32)
    marks = (ranks < counts[:, None]).reshape(BYTES)
    patch_index = (jnp.cumsum(marks.astype(jnp.int32)) - 1).astype(jnp.int32)
    positions = jnp.arange(BYTES, dtype=jnp.int32)
    starts = jnp.zeros((PATCHES,), jnp.int32).at[jnp.where(marks, patch_index, PATCHES)].set(positions, mode='drop')
    opens = jax.random.randint(doc_key, (PATCHES,), 0, PATCH_DEV) == 0
    opens = opens.at[0].set(True)
    doc_of_patch = lax.cummax(jnp.where(opens, starts, 0), axis=0)
    doc_begin = jnp.take(doc_of_patch, patch_index)
    return (starts, doc_begin)


def paired_weights(key, strength):
    first_key, second_key = jax.random.split(key)
    spread = strength / math.sqrt(DD)
    first = jnp.clip(jax.random.normal(first_key, (DD, DD), jnp.float32), -4.0, 4.0) * spread
    noise = jnp.clip(jax.random.normal(second_key, (DD, DD), jnp.float32), -4.0, 4.0) * spread
    second = noise
    return (jnp.clip(first, -2.0, 2.0), jnp.clip(second, -2.0, 2.0))


def draw_latent(key, part):
    return scaled_rows(jax.random.fold_in(key, 11), PATCHES, DL, 3.0).astype(jnp.bfloat16)


def draw_stream(key, part):
    return scaled_rows(jax.random.fold_in(key, 12), BYTES, DD, 1.0).astype(jnp.bfloat16)


def draw_patch_starts(key, part):
    return layout(key)[0]


def draw_doc_starts(key, part):
    return layout(key)[1]


def draw_self_query(key, part):
    return paired_weights(jax.random.fold_in(key, 31), 1.4)[0].astype(jnp.bfloat16)


def draw_self_key(key, part):
    return paired_weights(jax.random.fold_in(key, 31), 1.4)[1].astype(jnp.bfloat16)


def draw_cross_query(key, part):
    return paired_weights(jax.random.fold_in(key, 32), 1.4)[0].astype(jnp.bfloat16)


def draw_cross_key(key, part):
    return paired_weights(jax.random.fold_in(key, 32), 1.4)[1].astype(jnp.bfloat16)


def level_of(key, extent, cuts, least, largest):
    factor_of, own = 1.0, jax.random.fold_in(key, 6)
    for dim, blocks in cuts:
        heights = jnp.exp(jax.random.uniform(jax.random.fold_in(own, dim), (blocks,), jnp.float32, least / len(cuts), largest / len(cuts)))
        factor_of = factor_of * jnp.repeat(heights, extent[dim] // blocks).reshape([-1 if axis == dim else 1 for axis in range(len(extent))])
    return factor_of


def gaussian(key, extent, scale, limit, shards=(), kind=jnp.bfloat16):
    result = jax.random.normal(key, extent, jnp.float32) * scale
    if len(shards) > 0:
        result = level_of(key, extent, shards, -0.22, 0.18) * result
    return jnp.clip(result, min=-limit, max=limit).astype(kind)


def setup_inputs(seed: int = 0) -> dict:
    splits = jax.random.split(jax.random.key(seed), 16)
    latent = draw_latent(jax.random.fold_in(splits[15], 71), 0)
    latent_gain = jnp.clip(1.0 + 0.18 * jax.random.normal(splits[1], (DL,), jnp.float32), 0.099609375, 1.8984375).astype(jnp.bfloat16)
    proj_weight = gaussian(splits[2], (DL, DD), DL ** -0.5, 0.09375, ((0, 2),))
    patch_starts = draw_patch_starts(jax.random.fold_in(splits[15], 71), 0)
    stream = draw_stream(jax.random.fold_in(splits[15], 71), 0)
    doc_starts = draw_doc_starts(jax.random.fold_in(splits[15], 71), 0)
    stream_gain = jnp.clip(1.0 + 0.18 * jax.random.normal(splits[6], (DD,), jnp.float32), 0.099609375, 1.8984375).astype(jnp.bfloat16)
    self_query = draw_self_query(jax.random.fold_in(splits[15], 71), 0)
    self_key = draw_self_key(jax.random.fold_in(splits[15], 71), 0)
    self_value = gaussian(splits[9], (DD, DD), DD ** -0.5, 0.1875, ((1, 2),))
    self_out = gaussian(splits[10], (DD, DD), DD ** -0.5, 0.1875, ((0, 2),))
    cross_query = draw_cross_query(jax.random.fold_in(splits[15], 71), 0)
    cross_key = draw_cross_key(jax.random.fold_in(splits[15], 71), 0)
    cross_value = gaussian(splits[13], (DD, DD), DD ** -0.5, 0.1875, ((1, 2),))
    cross_out = gaussian(splits[14], (DD, DD), DD ** -0.5, 0.1875, ((0, 2),))
    return dict(latent=latent, latent_gain=latent_gain, proj_weight=proj_weight, patch_starts=patch_starts, stream=stream, doc_starts=doc_starts, stream_gain=stream_gain, self_query=self_query, self_key=self_key, self_value=self_value, self_out=self_out, cross_query=cross_query, cross_key=cross_key, cross_value=cross_value, cross_out=cross_out)


def norm_rows(values, gain):
    widened = values.astype(jnp.float32)
    mean_square = lax.optimization_barrier(jnp.mean(widened * widened, axis=1, keepdims=True))
    return (widened * lax.rsqrt(mean_square + 1e-05) * gain.astype(jnp.float32)).astype(jnp.bfloat16)

def project(left, right):
    return jnp.dot(left, right, preferred_element_type=jnp.float32).astype(jnp.bfloat16)

def attend(query, all_keys, all_values, allowed):
    row_count = query.shape[0]
    key_count = all_keys.shape[0]
    query_heads = query.reshape(row_count, HEADS, HD).astype(jnp.float32)
    key_heads = all_keys.reshape(key_count, HEADS, HD).astype(jnp.float32)
    value_heads = all_values.reshape(key_count, HEADS, HD).astype(jnp.float32)
    scores = jnp.einsum('rhd,khd->hrk', query_heads, key_heads) * HD ** (-0.5)
    scores = jnp.where(allowed[None], scores, -1e+30)
    row_max = lax.optimization_barrier(jnp.max(scores, axis=2, keepdims=True))
    weights = jnp.where(allowed[None], jnp.exp(scores - row_max), 0.0)
    row_total = lax.optimization_barrier(jnp.sum(weights, axis=2, keepdims=True))
    probs = (weights / row_total).astype(jnp.bfloat16).astype(jnp.float32)
    head_mix = jnp.einsum('hrk,khd->rhd', probs, value_heads)
    return head_mix.reshape(row_count, HEADS * HD).astype(jnp.bfloat16)

def reference(latent, latent_gain, proj_weight, patch_starts, stream, doc_starts, stream_gain, self_query, self_key, self_value, self_out, cross_query, cross_key, cross_value, cross_out):
    patch_rep = project(norm_rows(latent, latent_gain), proj_weight)
    patch_keys = project(patch_rep, cross_key)
    patch_values = project(patch_rep, cross_value)
    hidden = norm_rows(stream, stream_gain)
    own_query = project(hidden, self_query)
    own_key = project(hidden, self_key)
    own_value = project(hidden, self_value)
    cross_rows = project(hidden, cross_query)
    front = jnp.zeros((WIN, DD), jnp.bfloat16)
    key_padded = jnp.concatenate([front, own_key], axis=0)
    value_padded = jnp.concatenate([front, own_value], axis=0)
    tail = jnp.zeros((PMAX, DD), jnp.bfloat16)
    patch_key_padded = jnp.concatenate([patch_keys, tail], axis=0)
    patch_value_padded = jnp.concatenate([patch_values, tail], axis=0)
    start_padded = jnp.concatenate([patch_starts, jnp.full((PMAX,), BYTES, jnp.int32)], axis=0)

    def segment_work(segment):
        first_byte = (segment * BYTES_DEV).astype(jnp.int32)
        positions = first_byte + jnp.arange(BYTES_DEV, dtype=jnp.int32)
        key_pos = first_byte - WIN + jnp.arange(WIN + BYTES_DEV, dtype=jnp.int32)
        doc_rows = lax.dynamic_slice_in_dim(doc_starts, first_byte, BYTES_DEV)
        query_rows = lax.dynamic_slice_in_dim(own_query, first_byte, BYTES_DEV)
        near_keys = lax.dynamic_slice_in_dim(key_padded, first_byte, WIN + BYTES_DEV)
        near_values = lax.dynamic_slice_in_dim(value_padded, first_byte, WIN + BYTES_DEV)
        allowed = (key_pos[None, :] <= positions[:, None]) & (key_pos[None, :] >= positions[:, None] - WIN) & (key_pos[None, :] >= doc_rows[:, None])
        self_mixed = attend(query_rows, near_keys, near_values, allowed)
        offset = jnp.sum((patch_starts < first_byte - WIN).astype(jnp.int32)).astype(jnp.int32)
        slot_keys = lax.dynamic_slice_in_dim(patch_key_padded, offset, PMAX)
        slot_values = lax.dynamic_slice_in_dim(patch_value_padded, offset, PMAX)
        slot_starts = lax.dynamic_slice_in_dim(start_padded, offset, PMAX)
        cross_allowed = (slot_starts[None, :] <= positions[:, None]) & (slot_starts[None, :] >= doc_rows[:, None]) & (slot_starts[None, :] >= positions[:, None] - WIN)
        cross_query_rows = lax.dynamic_slice_in_dim(cross_rows, first_byte, BYTES_DEV)
        cross_mixed = attend(cross_query_rows, slot_keys, slot_values, cross_allowed)
        return (self_mixed, cross_mixed)
    self_all, cross_all = lax.map(segment_work, jnp.arange(N_SEQ, dtype=jnp.int32))
    self_all = self_all.reshape(BYTES, DD)
    cross_all = cross_all.reshape(BYTES, DD)
    update = jnp.dot(self_all, self_out, preferred_element_type=jnp.float32) + jnp.dot(cross_all, cross_out, preferred_element_type=jnp.float32)
    return update.astype(jnp.bfloat16)
```

```python
import functools

import jax
import jax.numpy as jnp
from jax import lax
from jax.experimental import pallas as pl
from jax.experimental.pallas import tpu as pltpu
from jax.sharding import PartitionSpec as P

HD = 64
WIN = 512
DRIFT = 32
LANES = 128
QB = 256
F32 = jnp.float32
BF16 = jnp.bfloat16
FAR = -1e30


def shift(array, axis, by):
    devices = lax.axis_size(axis)
    pairs = [(i, i + by) for i in range(devices) if 0 <= i + by < devices]
    return lax.ppermute(array, axis, pairs)


def swap(array):
    return lax.ppermute(array, "tp", [(0, 1), (1, 0)])


def norm_rows(values, gain):
    widened = values.astype(F32)
    mean_square = jnp.mean(widened * widened, axis=1, keepdims=True)
    return (widened * lax.rsqrt(mean_square + 1e-05) * gain.astype(F32)).astype(BF16)


def mm(left, right):
    return jnp.dot(left, right, preferred_element_type=F32)


def pair_attend(query, keys, values, bias):
    rows = query.shape[0]
    low = lax.broadcasted_iota(jnp.int32, (rows, LANES), 1) < HD
    zero = jnp.zeros_like(query)
    scaled = query * jnp.asarray(HD**-0.5, BF16)
    both = jnp.concatenate([jnp.where(low, scaled, zero), jnp.where(low, zero, scaled)], axis=0)
    scores = lax.dot_general(both, keys, (((1,), (1,)), ((), ())), preferred_element_type=F32)
    wide = jnp.concatenate([values, jnp.ones_like(values)], axis=1)
    mixed = []
    for half in range(2):
        one = scores[half * rows : (half + 1) * rows] + bias
        top = jnp.max(one, axis=1, keepdims=True)
        weights = jnp.exp(one - top).astype(BF16)
        total = mm(weights, wide)
        mixed.append(total[:, :LANES] / total[:, LANES:])
    return jnp.where(low, mixed[0], mixed[1]).astype(BF16)


def proj_kernel(stream, gain, wk, wv, wq, wc, k_out, v_out, q_out, c_out):
    hidden = norm_rows(stream[...], gain[...])
    for weight, out in ((wk, k_out), (wv, v_out), (wq, q_out), (wc, c_out)):
        out[...] = mm(hidden, weight[...]).astype(BF16)


def self_kernel(q, k, v, mine, other, gain, wk, wv, low_key, out, keys, values):
    step = pl.program_id(0)
    half = mine.shape[0]
    halo = 2 * half

    @pl.when(step == 0)
    def _():
        place = lax.axis_index("tp")
        for piece, at in ((mine, place), (other, 1 - place)):
            hidden = norm_rows(piece[...], gain[...])
            rows = pl.ds(pl.multiple_of(at * half, half), half)
            keys[rows, :] = mm(hidden, wk[...]).astype(BF16)
            values[rows, :] = mm(hidden, wv[...]).astype(BF16)
        keys[halo:, :] = k[...]
        values[halo:, :] = v[...]

    count = halo + QB
    base = pl.multiple_of(step * QB, QB)
    index = lax.broadcasted_iota(jnp.int32, (QB, count), 1)
    row = lax.broadcasted_iota(jnp.int32, (QB, count), 0)
    allowed = (index <= row + halo) & (index >= low_key[...] - base)
    bias = jnp.where(allowed, 0.0, FAR).astype(F32)
    for col in range(0, q.shape[1], LANES):
        cols = slice(col, col + LANES)
        out[:, cols] = pair_attend(
            q[:, cols], keys[pl.ds(base, count), cols], values[pl.ds(base, count), cols], bias
        )


def cross_kernel(
    q, rep, left_mine, left_other, right_mine, right_other, wk, wv, starts, low_key, mixed, ws, wc,
    own_out, far_out, joined, keys, values, cross,
):
    step = pl.program_id(0)
    place = lax.axis_index("tp")
    width = left_mine.shape[1]
    here = pl.ds(pl.multiple_of(place * width, width), width)
    there = pl.ds(pl.multiple_of((1 - place) * width, width), width)
    before, own, after = left_mine.shape[0], rep.shape[0], right_mine.shape[0]
    used = before + own + after

    @pl.when(step == 0)
    def _():
        joined[:before, here] = left_mine[...]
        joined[:before, there] = left_other[...]
        joined[before : before + own, :] = rep[...]
        joined[before + own :, here] = right_mine[...]
        joined[before + own :, there] = right_other[...]
        for weight, target in ((wk, keys), (wv, values)):
            target[:used, :] = mm(joined[...], weight[...]).astype(BF16)
            target[used:, :] = jnp.zeros((target.shape[0] - used, target.shape[1]), BF16)

    slots = keys.shape[0] - LANES
    per_win = WIN // QB
    base = pl.multiple_of(lax.rem(lax.div(step, per_win), 2) * LANES, LANES)
    index = starts[:, pl.ds(base, slots)]
    row = lax.broadcasted_iota(jnp.int32, (QB, slots), 0) + step * QB
    allowed = (index <= row) & (index >= low_key[...])
    bias = jnp.where(allowed, 0.0, FAR).astype(F32)
    for col in range(0, q.shape[1], LANES):
        cols = slice(col, col + LANES)
        cross[:, cols] = pair_attend(
            q[:, cols], keys[pl.ds(base, slots), cols], values[pl.ds(base, slots), cols], bias
        )
    own_out[...] = mm(mixed[...], ws[:, here]) + mm(cross[...], wc[:, here])
    far_out[...] = (mm(mixed[...], ws[:, there]) + mm(cross[...], wc[:, there])).astype(BF16)


def rows_spec(width):
    return pl.BlockSpec((QB, width), lambda i: (i, 0))


def whole(array):
    return pl.BlockSpec(array.shape, lambda i: (0,) * array.ndim)


def on_device(
    latent, latent_gain, proj_weight, patch_starts, stream, doc_starts, stream_gain,
    self_query, self_key, self_value, self_out, cross_query, cross_key, cross_value, cross_out,
):
    seg, width = stream.shape
    patch_dev = latent.shape[0]
    cols = self_query.shape[1]
    place = lax.axis_index("tp")
    seq_place = lax.axis_index("seq")
    steps = seg // QB
    gain = stream_gain[None, :]
    params = pltpu.CompilerParams(dimension_semantics=("arbitrary",), vmem_limit_bytes=48 << 20)

    half = WIN // 2
    tail = lax.dynamic_slice_in_dim(stream, seg - WIN + place * half, half, 0)
    halo_mine = shift(tail, "seq", 1)
    halo_other = swap(halo_mine)

    widened = latent.astype(F32)
    square = jnp.sum(widened * widened, axis=1)
    square_sum = square + swap(square)

    piece = jax.ShapeDtypeStruct((seg, cols), BF16)
    own_key, own_value, own_query, cross_rows = pl.pallas_call(
        proj_kernel,
        grid=(steps,),
        in_specs=[rows_spec(width), whole(gain)] + [whole(self_key)] * 4,
        out_specs=[rows_spec(cols)] * 4,
        out_shape=[piece] * 4,
        compiler_params=params,
        cost_estimate=pl.CostEstimate(flops=8 * seg * width * cols, bytes_accessed=12 << 20, transcendentals=0),
    )(stream, gain, self_key, self_value, self_query, cross_query)

    full_width = latent.shape[1] * lax.axis_size("tp")
    latent_normed = (
        widened * lax.rsqrt(square_sum / full_width + 1e-05)[:, None] * latent_gain.astype(F32)
    ).astype(BF16)
    partial = mm(latent_normed, proj_weight)
    rep = (partial + swap(partial)).astype(BF16)
    per_win = WIN * patch_dev // seg
    before, after = per_win + DRIFT, DRIFT
    share = lax.dynamic_slice_in_dim(rep, place * cols, cols, 1)
    left_mine = shift(share[patch_dev - before :], "seq", 1)
    right_mine = shift(share[:after], "seq", -1)
    arrived = swap(jnp.concatenate([left_mine, right_mine], axis=0))
    left_other, right_other = arrived[:before], arrived[before:]

    positions = jnp.arange(seg, dtype=jnp.int32)
    low_byte = jnp.maximum(positions - WIN, doc_starts - seq_place * seg)[:, None]
    low_spec = pl.BlockSpec((QB, 1), lambda i: (i, 0))
    self_mixed = pl.pallas_call(
        self_kernel,
        grid=(steps,),
        in_specs=[
            rows_spec(cols), whole(own_key), whole(own_key), whole(tail), whole(tail),
            whole(gain), whole(self_key), whole(self_key), low_spec,
        ],
        out_specs=rows_spec(cols),
        out_shape=piece,
        scratch_shapes=[pltpu.VMEM((WIN + seg, cols), BF16)] * 2,
        compiler_params=params,
        cost_estimate=pl.CostEstimate(flops=16 << 30, bytes_accessed=6 << 20, transcendentals=seg * 8 * 768),
    )(own_query, own_key, own_value, halo_mine, halo_other, gain, self_key, self_value, low_byte + WIN)

    used = before + patch_dev + after
    slots = (used + LANES - 1) // LANES * LANES
    padded = jnp.pad(
        patch_starts - seq_place * seg, (before, slots), constant_values=seg * (lax.axis_size("seq") + 1)
    )
    window = lax.dynamic_slice_in_dim(padded, seq_place * patch_dev, slots, 0)
    window = jnp.where(jnp.arange(slots) < used, window, seg)[None, :]
    own, far = pl.pallas_call(
        cross_kernel,
        grid=(steps,),
        in_specs=[
            rows_spec(cols), whole(rep), whole(left_mine), whole(left_mine), whole(right_mine), whole(right_mine),
            whole(cross_key), whole(cross_key), whole(window), low_spec, rows_spec(cols),
            whole(self_out), whole(cross_out),
        ],
        out_specs=[rows_spec(cols)] * 2,
        out_shape=[jax.ShapeDtypeStruct((seg, cols), F32), piece],
        scratch_shapes=[
            pltpu.VMEM((used, width), BF16), pltpu.VMEM((slots, cols), BF16),
            pltpu.VMEM((slots, cols), BF16), pltpu.VMEM((QB, cols), BF16),
        ],
        compiler_params=params,
        cost_estimate=pl.CostEstimate(flops=10 << 30, bytes_accessed=8 << 20, transcendentals=seg * 8 * 384),
    )(
        cross_rows, rep, left_mine, left_other, right_mine, right_other, cross_key, cross_value,
        window, low_byte, self_mixed, self_out, cross_out,
    )
    return (own + swap(far).astype(F32)).astype(BF16)


def solution(mesh):
    in_specs = (
        P("seq", "tp"), P("tp"), P("tp", None), P(), P("seq", None), P("seq"), P(),
        P(None, "tp"), P(None, "tp"), P(None, "tp"), P("tp", None),
        P(None, "tp"), P(None, "tp"), P(None, "tp"), P("tp", None),
    )
    return jax.shard_map(
        on_device, mesh=mesh, in_specs=in_specs, out_specs=P("seq", "tp"), check_vma=False
    )
```

```python
import jax
import jax.numpy as jnp
from jax import lax
from jax.experimental import pallas as pl
from jax.experimental.pallas import tpu as pltpu
from jax.sharding import PartitionSpec as P

HD = 64
WIN = 512
PMAX = 448
DRIFT = 32
LANES = 128
QB = 256
F32 = jnp.float32
BF16 = jnp.bfloat16
FAR = -1e30
MESH = pl.DeviceIdType.MESH


def norm_rows(values, gain):
    widened = values.astype(F32)
    mean_square = jnp.mean(widened * widened, axis=1, keepdims=True)
    return (widened * lax.rsqrt(mean_square + 1e-05) * gain.astype(F32)).astype(BF16)


def mm(left, right):
    return jnp.dot(left, right, preferred_element_type=F32)


def pair_attend(query, keys, values, bias):
    rows = query.shape[0]
    low = lax.broadcasted_iota(jnp.int32, (rows, LANES), 1) < HD
    zero = jnp.zeros_like(query)
    scaled = query * jnp.asarray(HD**-0.5, BF16)
    both = jnp.concatenate([jnp.where(low, scaled, zero), jnp.where(low, zero, scaled)], axis=0)
    scores = lax.dot_general(both, keys, (((1,), (1,)), ((), ())), preferred_element_type=F32)
    wide = jnp.concatenate([values, jnp.ones_like(values)], axis=1)
    mixed = []
    for half in range(2):
        one = scores[half * rows : (half + 1) * rows] + bias
        top = jnp.max(one, axis=1, keepdims=True)
        weights = jnp.exp(one - top).astype(BF16)
        total = mm(weights, wide)
        mixed.append(total[:, :LANES] / total[:, LANES:])
    return jnp.where(low, mixed[0], mixed[1]).astype(BF16)


def from_behind(array, axis, by):
    devices = lax.axis_size(axis)
    pairs = [(i, i + by) for i in range(devices) if 0 <= i + by < devices]
    return lax.ppermute(array, axis, pairs)


def project(left, right):
    return jnp.dot(left, right, preferred_element_type=jnp.float32).astype(jnp.bfloat16)


def attend(query, all_keys, all_values, allowed, head_size):
    row_count = query.shape[0]
    key_count = all_keys.shape[0]
    head_count = query.shape[1] // head_size
    query_heads = query.reshape(row_count, head_count, head_size)
    key_heads = all_keys.reshape(key_count, head_count, head_size)
    value_heads = all_values.reshape(key_count, head_count, head_size)
    scores = jnp.einsum(
        "rhd,khd->hrk", query_heads, key_heads, preferred_element_type=jnp.float32
    ) * head_size ** (-0.5)
    scores = jnp.where(allowed[None], scores, -1e30)
    row_max = jnp.max(scores, axis=2, keepdims=True)
    weights = jnp.where(allowed[None], jnp.exp(scores - row_max), 0.0)
    row_total = jnp.sum(weights, axis=2, keepdims=True)
    probs = (weights / row_total).astype(jnp.bfloat16)
    head_mix = jnp.einsum("hrk,khd->rhd", probs, value_heads, preferred_element_type=jnp.float32)
    return head_mix.reshape(row_count, head_count * head_size).astype(jnp.bfloat16)


def general_device(
    latent,
    latent_gain,
    proj_weight,
    patch_starts,
    stream,
    doc_starts,
    stream_gain,
    self_query,
    self_key,
    self_value,
    self_out,
    cross_query,
    cross_key,
    cross_value,
    cross_out,
):
    seg_bytes = stream.shape[0]
    patch_dev = latent.shape[0]
    slot_count = PMAX
    seq_place = lax.axis_index("seq")
    first_byte = seq_place * seg_bytes
    total_bytes = seg_bytes * lax.axis_size("seq")
    head_size = HD
    widened = latent.astype(jnp.float32)
    square_sum = lax.psum(jnp.sum(widened * widened, axis=1), "tp")
    full_width = latent.shape[1] * lax.axis_size("tp")
    latent_normed = (
        widened
        * lax.rsqrt(square_sum / full_width + 1e-05)[:, None]
        * latent_gain.astype(jnp.float32)
    ).astype(jnp.bfloat16)
    partial_value = jnp.dot(latent_normed, proj_weight, preferred_element_type=jnp.float32)
    offset = jnp.sum((patch_starts < first_byte - WIN).astype(jnp.int32))
    anchor = offset - (seq_place - 1) * patch_dev
    rep_share = lax.psum_scatter(partial_value, "tp", scatter_dimension=1, tiled=True).astype(
        jnp.bfloat16
    )
    arrived = [from_behind(rep_share, "seq", towards) for towards in (1, -1)]
    joined = jnp.concatenate([arrived[0], rep_share, arrived[1]], axis=0)
    own_rows = lax.dynamic_slice_in_dim(joined, anchor, slot_count, 0)
    block_piece = lax.all_gather(own_rows, "tp", axis=1, tiled=True)
    key_total = jnp.dot(block_piece, cross_key, preferred_element_type=jnp.float32)
    value_total = jnp.dot(block_piece, cross_value, preferred_element_type=jnp.float32)
    patch_keys = key_total.astype(jnp.bfloat16)
    patch_values = value_total.astype(jnp.bfloat16)
    hidden = norm_rows(stream, stream_gain)
    own_query = project(hidden, self_query)
    own_key = project(hidden, self_key)
    own_value = project(hidden, self_value)
    cross_rows = project(hidden, cross_query)
    tail_rows = jnp.stack([own_key[seg_bytes - WIN :], own_value[seg_bytes - WIN :]])
    halo_rows = from_behind(tail_rows, "seq", 1)
    near_keys = jnp.concatenate([halo_rows[0], own_key], axis=0)
    near_values = jnp.concatenate([halo_rows[1], own_value], axis=0)
    positions = first_byte + jnp.arange(seg_bytes, dtype=jnp.int32)
    key_pos = first_byte - WIN + jnp.arange(WIN + seg_bytes, dtype=jnp.int32)
    allowed = (
        (key_pos[None, :] <= positions[:, None])
        & (key_pos[None, :] >= positions[:, None] - WIN)
        & (key_pos[None, :] >= doc_starts[:, None])
    )
    self_mixed = attend(own_query, near_keys, near_values, allowed, head_size)
    patch_total = patch_starts.shape[0]
    slot_index = offset + jnp.arange(slot_count, dtype=jnp.int32)
    slot_starts = jnp.where(
        slot_index < patch_total,
        jnp.take(patch_starts, jnp.minimum(slot_index, patch_total - 1)),
        total_bytes,
    )
    cross_allowed = (
        (slot_starts[None, :] <= positions[:, None])
        & (slot_starts[None, :] >= doc_starts[:, None])
        & (slot_starts[None, :] >= positions[:, None] - WIN)
    )
    cross_mixed = attend(cross_rows, patch_keys, patch_values, cross_allowed, head_size)
    partial_out = jnp.dot(self_mixed, self_out, preferred_element_type=jnp.float32) + jnp.dot(
        cross_mixed, cross_out, preferred_element_type=jnp.float32
    )
    return lax.psum_scatter(partial_out.astype(jnp.bfloat16), "tp", scatter_dimension=1, tiled=True)


def layer_kernel(
    latent_h, proj_h, stream_h, wk_h, wv_h, wq_h, wc_h, ck_h, cv_h, so_h, co_h,
    latent_gain, gain, starts, low_key, out,
    latent, proj, stream, wk, wv, wq, wc, ck, cv, so, co,
    halo, keys, values, queries, cross_rows, mixed, cross, sq_mine, sq_peer, part_mine, part_peer,
    joined, patch_keys, patch_values, own, far, far_peer, local_sem, send_sem, recv_sem,
):
    seg, width = stream.shape
    cols = wk.shape[1]
    patch_dev = latent.shape[0]
    place, place_seq = lax.axis_index("tp"), lax.axis_index("seq")
    last = lax.axis_size("seq") - 1
    peer = {"tp": 1 - place}
    right, left = {"seq": jnp.minimum(place_seq + 1, last)}, {"seq": jnp.maximum(place_seq - 1, 0)}
    has_left, has_right = place_seq > 0, place_seq < last
    here = pl.ds(pl.multiple_of(place * cols, cols), cols)
    there = pl.ds(pl.multiple_of((1 - place) * cols, cols), cols)

    pairs = (
        (latent_h, latent), (stream_h, stream), (wk_h, wk), (wv_h, wv), (wq_h, wq), (wc_h, wc),
        (proj_h, proj), (ck_h, ck), (cv_h, cv), (so_h, so), (co_h, co),
    )
    loads = [pltpu.make_async_copy(a, b, local_sem.at[i]) for i, (a, b) in enumerate(pairs)]
    for load in loads:
        load.start()

    barrier = pltpu.get_barrier_semaphore()
    pl.semaphore_signal(barrier, inc=1, device_id=peer, device_id_type=MESH)

    @pl.when(has_left)
    def _():
        pl.semaphore_signal(barrier, inc=1, device_id=left, device_id_type=MESH)

    @pl.when(has_right)
    def _():
        pl.semaphore_signal(barrier, inc=1, device_id=right, device_id_type=MESH)

    pl.semaphore_wait(barrier, 1 + has_left.astype(jnp.int32) + has_right.astype(jnp.int32))

    def send(source, target, index, to):
        return pltpu.make_async_remote_copy(
            src_ref=source, dst_ref=target, send_sem=send_sem.at[index], recv_sem=recv_sem.at[index],
            device_id=to, device_id_type=MESH,
        )

    half = WIN // 2
    mine = pl.ds(pl.multiple_of(place * half, half), half)
    tail = pl.ds(pl.multiple_of(seg - WIN + place * half, half), half)
    halo_send = send(stream_h.at[tail, :], halo.at[mine, :], 0, right)
    halo_swap = send(halo.at[mine, :], halo.at[mine, :], 1, peer)
    sq_swap = send(sq_mine, sq_peer, 2, peer)
    part_swap = send(part_mine, part_peer, 3, peer)
    after = DRIFT
    before = joined.shape[0] - patch_dev - after
    front, back = pl.ds(0, before), pl.ds(before + patch_dev, after)
    rep_right = send(joined.at[pl.ds(patch_dev, before), here], joined.at[front, here], 4, right)
    rep_left = send(joined.at[pl.ds(before, after), here], joined.at[back, here], 5, left)
    front_swap = send(joined.at[front, here], joined.at[front, here], 6, peer)
    back_swap = send(joined.at[back, here], joined.at[back, here], 7, peer)

    @pl.when(has_right)
    def _():
        halo_send.start()

    loads[0].wait()
    widened = latent[...].astype(F32)
    square = jnp.sum(widened * widened, axis=1, keepdims=True)
    sq_mine[...] = jnp.broadcast_to(square, sq_mine.shape)
    sq_swap.start()

    for load in loads[1:6]:
        load.wait()

    def project_rows(step, carry):
        rows = pl.ds(pl.multiple_of(step * QB, QB), QB)
        shifted = pl.ds(pl.multiple_of(step * QB + WIN, QB), QB)
        hidden = norm_rows(stream[rows, :], gain[...])
        keys[shifted, :] = mm(hidden, wk[...]).astype(BF16)
        values[shifted, :] = mm(hidden, wv[...]).astype(BF16)
        queries[rows, :] = mm(hidden, wq[...]).astype(BF16)
        cross_rows[rows, :] = mm(hidden, wc[...]).astype(BF16)
        return carry

    lax.fori_loop(0, seg // QB, project_rows, 0)

    loads[6].wait()
    sq_swap.wait()
    scale = lax.rsqrt((sq_mine[:, :1] + sq_peer[:, :1]) / (2 * latent.shape[1]) + 1e-05)
    normed = (latent[...].astype(F32) * scale * latent_gain[...].astype(F32)).astype(BF16)
    part_mine[...] = mm(normed, proj[...])
    part_swap.start()

    count = WIN + QB
    index = lax.broadcasted_iota(jnp.int32, (QB, count), 1)
    row = lax.broadcasted_iota(jnp.int32, (QB, count), 0)

    def self_rows(step, carry):
        base = pl.multiple_of(step * QB, QB)
        rows, near = pl.ds(base, QB), pl.ds(base, count)
        allowed = (index <= row + WIN) & (index >= low_key[rows, :] + (WIN - base))
        bias = jnp.where(allowed, 0.0, FAR).astype(F32)
        for col in range(0, cols, LANES):
            at = slice(col, col + LANES)
            mixed[rows, at] = pair_attend(queries[rows, at], keys[near, at], values[near, at], bias)
        return carry

    inner = WIN // QB
    lax.fori_loop(inner, inner + 1, self_rows, 0)

    part_swap.wait()
    joined[pl.ds(before, patch_dev), :] = (part_mine[...] + part_peer[...]).astype(BF16)

    @pl.when(has_right)
    def _():
        rep_right.start()
        halo_send.wait_send()

    @pl.when(has_left)
    def _():
        rep_left.start()
        halo_send.wait_recv()
        halo_swap.start()

    lax.fori_loop(inner + 1, seg // QB, self_rows, 0)

    @pl.when(has_right)
    def _():
        rep_right.wait_send()
        rep_left.wait_recv()
        back_swap.start()

    @pl.when(has_left)
    def _():
        rep_left.wait_send()
        rep_right.wait_recv()
        front_swap.start()
        halo_swap.wait()

    @pl.when(jnp.logical_not(has_left))
    def _():
        halo[...] = jnp.zeros_like(halo)
        joined[front, :] = jnp.zeros((before, width), BF16)

    @pl.when(jnp.logical_not(has_right))
    def _():
        joined[back, :] = jnp.zeros((after, width), BF16)

    hidden = norm_rows(halo[...], gain[...])
    keys[:WIN, :] = mm(hidden, wk[...]).astype(BF16)
    values[:WIN, :] = mm(hidden, wv[...]).astype(BF16)
    lax.fori_loop(0, inner, self_rows, 0)

    @pl.when(has_right)
    def _():
        back_swap.wait()

    @pl.when(has_left)
    def _():
        front_swap.wait()

    for load in loads[7:]:
        load.wait()
    used = joined.shape[0]
    for weight, target in ((ck, patch_keys), (cv, patch_values)):
        target[:used, :] = mm(joined[...], weight[...]).astype(BF16)
        target[used:, :] = jnp.zeros((target.shape[0] - used, cols), BF16)

    slots = patch_keys.shape[0] - LANES
    slot_row = lax.broadcasted_iota(jnp.int32, (QB, slots), 0)

    def out_swap(step):
        rows = pl.ds(pl.multiple_of(step * QB, QB), QB)
        return send(far.at[rows, :], far_peer.at[rows, :], 8 + step, peer)

    def finish(step):
        out_swap(step).wait()
        rows = pl.ds(pl.multiple_of(step * QB, QB), QB)
        out[rows, :] = (own[rows, :] + far_peer[rows, :].astype(F32)).astype(BF16)

    def cross_block(step, carry):
        rows = pl.ds(pl.multiple_of(step * QB, QB), QB)
        base = pl.multiple_of(lax.rem(lax.div(step, inner), 2) * LANES, LANES)
        near = pl.ds(base, slots)
        first = starts[:, near]
        allowed = (first <= slot_row + step * QB) & (first >= low_key[rows, :])
        bias = jnp.where(allowed, 0.0, FAR).astype(F32)
        for col in range(0, cols, LANES):
            at = slice(col, col + LANES)
            cross[:, at] = pair_attend(
                cross_rows[rows, at], patch_keys[near, at], patch_values[near, at], bias
            )
        far[rows, :] = (mm(mixed[rows, :], so[:, there]) + mm(cross[...], co[:, there])).astype(BF16)
        out_swap(step).start()
        own[rows, :] = mm(mixed[rows, :], so[:, here]) + mm(cross[...], co[:, here])

        @pl.when(step > 0)
        def _():
            finish(step - 1)

        return carry

    lax.fori_loop(0, seg // QB, cross_block, 0)
    finish(seg // QB - 1)


def pair_device(
    latent, latent_gain, proj_weight, patch_starts, stream, doc_starts, stream_gain,
    self_query, self_key, self_value, self_out, cross_query, cross_key, cross_value, cross_out,
):
    seg, width = stream.shape
    patch_dev, features = latent.shape
    cols = self_query.shape[1]
    first_byte = lax.axis_index("seq") * seg
    before, after = WIN * patch_dev // seg + DRIFT, DRIFT
    used = before + patch_dev + after
    slots = (used + LANES - 1) // LANES * LANES

    positions = jnp.arange(seg, dtype=jnp.int32)
    low_byte = jnp.maximum(positions - WIN, doc_starts - first_byte)[:, None]
    padded = jnp.pad(
        patch_starts - first_byte, (before, slots), constant_values=seg * (lax.axis_size("seq") + 1)
    )
    window = lax.dynamic_slice_in_dim(padded, lax.axis_index("seq") * patch_dev, slots, 0)
    window = jnp.where(jnp.arange(slots) < used, window, seg)[None, :]

    big = (latent, proj_weight, stream, self_key, self_value, self_query, cross_query, cross_key, cross_value, self_out, cross_out)
    small = (latent_gain[None, :], stream_gain[None, :], window, low_byte)
    blocks = seg // QB
    return pl.pallas_call(
        layer_kernel,
        in_specs=[pl.BlockSpec(memory_space=pl.ANY)] * len(big)
        + [pl.BlockSpec(memory_space=pltpu.VMEM)] * len(small),
        out_specs=pl.BlockSpec(memory_space=pltpu.VMEM),
        out_shape=jax.ShapeDtypeStruct((seg, cols), BF16),
        scratch_shapes=[pltpu.VMEM(array.shape, BF16) for array in big]
        + [
            pltpu.VMEM((WIN, width), BF16),
            pltpu.VMEM((WIN + seg, cols), BF16),
            pltpu.VMEM((WIN + seg, cols), BF16),
            pltpu.VMEM((seg, cols), BF16),
            pltpu.VMEM((seg, cols), BF16),
            pltpu.VMEM((seg, cols), BF16),
            pltpu.VMEM((QB, cols), BF16),
            pltpu.VMEM((patch_dev, LANES), F32),
            pltpu.VMEM((patch_dev, LANES), F32),
            pltpu.VMEM((patch_dev, width), F32),
            pltpu.VMEM((patch_dev, width), F32),
            pltpu.VMEM((used, width), BF16),
            pltpu.VMEM((slots, cols), BF16),
            pltpu.VMEM((slots, cols), BF16),
            pltpu.VMEM((seg, cols), F32),
            pltpu.VMEM((seg, cols), BF16),
            pltpu.VMEM((seg, cols), BF16),
            pltpu.SemaphoreType.DMA((len(big),)),
            pltpu.SemaphoreType.DMA((8 + blocks,)),
            pltpu.SemaphoreType.DMA((8 + blocks,)),
        ],
        compiler_params=pltpu.CompilerParams(
            collective_id=0, has_side_effects=True, vmem_limit_bytes=60 << 20
        ),
    )(*big, *small)


def solution(mesh):
    in_specs = (
        P("seq", "tp"), P("tp"), P("tp", None), P(), P("seq", None), P("seq"), P(),
        P(None, "tp"), P(None, "tp"), P(None, "tp"), P("tp", None),
        P(None, "tp"), P(None, "tp"), P(None, "tp"), P("tp", None),
    )
    return jax.shard_map(
        pair_device if mesh.shape["tp"] == 2 else general_device, mesh=mesh, in_specs=in_specs, out_specs=P("seq", "tp"), check_vma=False
    )
```

```python
import jax
import jax.numpy as jnp
from jax import lax
from jax.experimental import pallas as pl
from jax.experimental.pallas import tpu as pltpu
from jax.sharding import PartitionSpec as P

HD = 64
WIN = 512
PMAX = 448
DRIFT = 32
LANES = 128
QB = 256
F32 = jnp.float32
BF16 = jnp.bfloat16
FAR = -1e30
MESH = pl.DeviceIdType.MESH


def norm_rows(values, gain):
    widened = values.astype(F32)
    mean_square = jnp.mean(widened * widened, axis=1, keepdims=True)
    return (widened * lax.rsqrt(mean_square + 1e-05) * gain.astype(F32)).astype(BF16)


def mm(left, right):
    return jnp.dot(left, right, preferred_element_type=F32)


def score_pair(query, keys):
    low = lax.broadcasted_iota(jnp.int32, query.shape, 1) < HD
    zero = jnp.zeros_like(query)
    scaled = query * jnp.asarray(HD**-0.5, BF16)
    both = jnp.concatenate([jnp.where(low, scaled, zero), jnp.where(low, zero, scaled)], axis=0)
    return lax.dot_general(both, keys, (((1,), (1,)), ((), ())), preferred_element_type=F32)


def mix_pair(scores, values, bias):
    rows = bias.shape[0]
    wide = jnp.concatenate([values, jnp.ones_like(values)], axis=1)
    totals = []
    for part in range(2):
        one = scores[part * rows : (part + 1) * rows] + bias
        top = jnp.max(one, axis=1, keepdims=True)
        totals.append(mm(jnp.exp(one - top).astype(BF16), wide))
    low = lax.broadcasted_iota(jnp.int32, (rows, LANES), 1) < HD
    upper = jnp.where(low, totals[0][:, :LANES], totals[1][:, :LANES])
    lower = jnp.where(low, totals[0][:, LANES:], totals[1][:, LANES:])
    return (upper / lower).astype(BF16)


def attend_pairs(query, rows, keys, values, near, bias, out, out_rows):
    places = [slice(col, col + LANES) for col in range(0, query.shape[1], LANES)]
    scores = score_pair(query[rows, places[0]], keys[near, places[0]])
    for number, at in enumerate(places):
        ready = scores
        if number + 1 < len(places):
            ahead = places[number + 1]
            scores = score_pair(query[rows, ahead], keys[near, ahead])
        out[out_rows, at] = mix_pair(ready, values[near, at], bias)


def from_behind(array, axis, by):
    devices = lax.axis_size(axis)
    pairs = [(i, i + by) for i in range(devices) if 0 <= i + by < devices]
    return lax.ppermute(array, axis, pairs)


def project(left, right):
    return jnp.dot(left, right, preferred_element_type=jnp.float32).astype(jnp.bfloat16)


def attend(query, all_keys, all_values, allowed, head_size):
    row_count = query.shape[0]
    key_count = all_keys.shape[0]
    head_count = query.shape[1] // head_size
    query_heads = query.reshape(row_count, head_count, head_size)
    key_heads = all_keys.reshape(key_count, head_count, head_size)
    value_heads = all_values.reshape(key_count, head_count, head_size)
    scores = jnp.einsum(
        "rhd,khd->hrk", query_heads, key_heads, preferred_element_type=jnp.float32
    ) * head_size ** (-0.5)
    scores = jnp.where(allowed[None], scores, -1e30)
    row_max = jnp.max(scores, axis=2, keepdims=True)
    weights = jnp.where(allowed[None], jnp.exp(scores - row_max), 0.0)
    row_total = jnp.sum(weights, axis=2, keepdims=True)
    probs = (weights / row_total).astype(jnp.bfloat16)
    head_mix = jnp.einsum("hrk,khd->rhd", probs, value_heads, preferred_element_type=jnp.float32)
    return head_mix.reshape(row_count, head_count * head_size).astype(jnp.bfloat16)


def general_device(
    latent,
    latent_gain,
    proj_weight,
    patch_starts,
    stream,
    doc_starts,
    stream_gain,
    self_query,
    self_key,
    self_value,
    self_out,
    cross_query,
    cross_key,
    cross_value,
    cross_out,
):
    seg_bytes = stream.shape[0]
    patch_dev = latent.shape[0]
    slot_count = PMAX
    seq_place = lax.axis_index("seq")
    first_byte = seq_place * seg_bytes
    total_bytes = seg_bytes * lax.axis_size("seq")
    head_size = HD
    widened = latent.astype(jnp.float32)
    square_sum = lax.psum(jnp.sum(widened * widened, axis=1), "tp")
    full_width = latent.shape[1] * lax.axis_size("tp")
    latent_normed = (
        widened
        * lax.rsqrt(square_sum / full_width + 1e-05)[:, None]
        * latent_gain.astype(jnp.float32)
    ).astype(jnp.bfloat16)
    partial_value = jnp.dot(latent_normed, proj_weight, preferred_element_type=jnp.float32)
    offset = jnp.sum((patch_starts < first_byte - WIN).astype(jnp.int32))
    anchor = offset - (seq_place - 1) * patch_dev
    rep_share = lax.psum_scatter(partial_value, "tp", scatter_dimension=1, tiled=True).astype(
        jnp.bfloat16
    )
    arrived = [from_behind(rep_share, "seq", towards) for towards in (1, -1)]
    joined = jnp.concatenate([arrived[0], rep_share, arrived[1]], axis=0)
    own_rows = lax.dynamic_slice_in_dim(joined, anchor, slot_count, 0)
    block_piece = lax.all_gather(own_rows, "tp", axis=1, tiled=True)
    key_total = jnp.dot(block_piece, cross_key, preferred_element_type=jnp.float32)
    value_total = jnp.dot(block_piece, cross_value, preferred_element_type=jnp.float32)
    patch_keys = key_total.astype(jnp.bfloat16)
    patch_values = value_total.astype(jnp.bfloat16)
    hidden = norm_rows(stream, stream_gain)
    own_query = project(hidden, self_query)
    own_key = project(hidden, self_key)
    own_value = project(hidden, self_value)
    cross_rows = project(hidden, cross_query)
    tail_rows = jnp.stack([own_key[seg_bytes - WIN :], own_value[seg_bytes - WIN :]])
    halo_rows = from_behind(tail_rows, "seq", 1)
    near_keys = jnp.concatenate([halo_rows[0], own_key], axis=0)
    near_values = jnp.concatenate([halo_rows[1], own_value], axis=0)
    positions = first_byte + jnp.arange(seg_bytes, dtype=jnp.int32)
    key_pos = first_byte - WIN + jnp.arange(WIN + seg_bytes, dtype=jnp.int32)
    allowed = (
        (key_pos[None, :] <= positions[:, None])
        & (key_pos[None, :] >= positions[:, None] - WIN)
        & (key_pos[None, :] >= doc_starts[:, None])
    )
    self_mixed = attend(own_query, near_keys, near_values, allowed, head_size)
    patch_total = patch_starts.shape[0]
    slot_index = offset + jnp.arange(slot_count, dtype=jnp.int32)
    slot_starts = jnp.where(
        slot_index < patch_total,
        jnp.take(patch_starts, jnp.minimum(slot_index, patch_total - 1)),
        total_bytes,
    )
    cross_allowed = (
        (slot_starts[None, :] <= positions[:, None])
        & (slot_starts[None, :] >= doc_starts[:, None])
        & (slot_starts[None, :] >= positions[:, None] - WIN)
    )
    cross_mixed = attend(cross_rows, patch_keys, patch_values, cross_allowed, head_size)
    partial_out = jnp.dot(self_mixed, self_out, preferred_element_type=jnp.float32) + jnp.dot(
        cross_mixed, cross_out, preferred_element_type=jnp.float32
    )
    return lax.psum_scatter(partial_out.astype(jnp.bfloat16), "tp", scatter_dimension=1, tiled=True)


def layer_kernel(
    latent_h, proj_h, stream_h, wk_h, wv_h, wq_h, wc_h, ck_h, cv_h, so_h, co_h,
    latent_gain, gain, patch_starts, doc_starts, out,
    latent, proj, stream, wk, wv, wq, wc, ck, cv, so, co,
    halo, keys, values, queries, cross_rows, mixed, cross, sq_mine, sq_peer, part_mine, part_peer,
    joined, patch_keys, patch_values, own, far, far_peer, starts, low_key, local_sem, send_sem, recv_sem,
):
    seg, width = stream.shape
    cols = wk.shape[1]
    patch_dev = latent.shape[0]
    place, place_seq = lax.axis_index("tp"), lax.axis_index("seq")
    last = lax.axis_size("seq") - 1
    peer = {"tp": 1 - place}
    right, left = {"seq": jnp.minimum(place_seq + 1, last)}, {"seq": jnp.maximum(place_seq - 1, 0)}
    has_left, has_right = place_seq > 0, place_seq < last
    here = pl.ds(pl.multiple_of(place * cols, cols), cols)
    there = pl.ds(pl.multiple_of((1 - place) * cols, cols), cols)

    pairs = (
        (latent_h, latent), (stream_h, stream), (wk_h, wk), (wv_h, wv), (wq_h, wq), (wc_h, wc),
        (proj_h, proj), (ck_h, ck), (cv_h, cv), (so_h, so), (co_h, co),
    )
    loads = [pltpu.make_async_copy(a, b, local_sem.at[i]) for i, (a, b) in enumerate(pairs)]
    for load in loads[:6]:
        load.start()

    barrier = pltpu.get_barrier_semaphore()
    pl.semaphore_signal(barrier, inc=1, device_id=peer, device_id_type=MESH)

    @pl.when(has_left)
    def _():
        pl.semaphore_signal(barrier, inc=1, device_id=left, device_id_type=MESH)

    @pl.when(has_right)
    def _():
        pl.semaphore_signal(barrier, inc=1, device_id=right, device_id_type=MESH)

    pl.semaphore_wait(barrier, 1 + has_left.astype(jnp.int32) + has_right.astype(jnp.int32))

    def send(source, target, index, to):
        return pltpu.make_async_remote_copy(
            src_ref=source, dst_ref=target, send_sem=send_sem.at[index], recv_sem=recv_sem.at[index],
            device_id=to, device_id_type=MESH,
        )

    half = WIN // 2
    mine = pl.ds(pl.multiple_of(place * half, half), half)
    tail = pl.ds(pl.multiple_of(seg - WIN + place * half, half), half)
    halo_send = send(stream_h.at[tail, :], halo.at[mine, :], 0, right)
    halo_swap = send(halo.at[mine, :], halo.at[mine, :], 1, peer)
    sq_swap = send(sq_mine, sq_peer, 2, peer)
    part_swap = send(part_mine, part_peer, 3, peer)
    after = DRIFT
    before = joined.shape[0] - patch_dev - after
    front, back = pl.ds(0, before), pl.ds(before + patch_dev, after)
    rep_right = send(joined.at[pl.ds(patch_dev, before), here], joined.at[front, here], 4, right)
    rep_left = send(joined.at[pl.ds(before, after), here], joined.at[back, here], 5, left)
    front_swap = send(joined.at[front, here], joined.at[front, here], 6, peer)
    back_swap = send(joined.at[back, here], joined.at[back, here], 7, peer)

    @pl.when(has_right)
    def _():
        halo_send.start()

    first_byte = place_seq * seg
    byte = lax.broadcasted_iota(jnp.int32, (LANES, LANES), 1)
    for at in range(0, seg, LANES):
        lowest = jnp.maximum(byte + (at - WIN), doc_starts[:, at : at + LANES] - first_byte)
        low_key[at : at + LANES, :] = lowest.T
    behind = pl.ds(pl.multiple_of(jnp.maximum(place_seq - 1, 0) * patch_dev, LANES), patch_dev)
    own_patches = pl.ds(pl.multiple_of(place_seq * patch_dev, LANES), patch_dev)
    ahead = pl.ds(pl.multiple_of(jnp.minimum(place_seq + 1, last) * patch_dev, LANES), LANES)
    tight = jnp.concatenate(
        [
            jnp.where(has_left, patch_starts[:, behind] - first_byte, seg),
            patch_starts[:, own_patches] - first_byte,
            jnp.where(has_right, patch_starts[:, ahead] - first_byte, seg),
        ],
        axis=1,
    )
    span = tight.shape[1]
    skipped = patch_dev - before
    tight = pltpu.roll(jnp.broadcast_to(tight, (8, span)), span - skipped, 1)[:, : starts.shape[1]]
    slot = lax.broadcasted_iota(jnp.int32, tight.shape, 1)
    starts[...] = jnp.where(slot < joined.shape[0], tight, seg)

    loads[0].wait()
    widened = latent[...].astype(F32)
    square = jnp.sum(widened * widened, axis=1, keepdims=True)
    sq_mine[...] = jnp.broadcast_to(square, sq_mine.shape)
    sq_swap.start()

    for load in loads[1:6]:
        load.wait()
    for load in loads[6:]:
        load.start()

    def project_rows(step, carry):
        rows = pl.ds(pl.multiple_of(step * QB, QB), QB)
        shifted = pl.ds(pl.multiple_of(step * QB + WIN, QB), QB)
        hidden = norm_rows(stream[rows, :], gain[...][None, :])
        keys[shifted, :] = mm(hidden, wk[...]).astype(BF16)
        values[shifted, :] = mm(hidden, wv[...]).astype(BF16)
        queries[rows, :] = mm(hidden, wq[...]).astype(BF16)
        cross_rows[rows, :] = mm(hidden, wc[...]).astype(BF16)
        return carry

    lax.fori_loop(0, seg // QB, project_rows, 0)

    loads[6].wait()
    sq_swap.wait()
    scale = lax.rsqrt((sq_mine[:, :1] + sq_peer[:, :1]) / (2 * latent.shape[1]) + 1e-05)
    normed = (latent[...].astype(F32) * scale * latent_gain[...][None, :].astype(F32)).astype(BF16)
    part_mine[...] = mm(normed, proj[...])
    part_swap.start()

    count = WIN + QB
    index = lax.broadcasted_iota(jnp.int32, (QB, count), 1)
    row = lax.broadcasted_iota(jnp.int32, (QB, count), 0)

    def self_rows(step, carry):
        base = pl.multiple_of(step * QB, QB)
        rows, near = pl.ds(base, QB), pl.ds(base, count)
        allowed = (index <= row + WIN) & (index >= low_key[rows, :1] + (WIN - base))
        bias = jnp.where(allowed, 0.0, FAR).astype(F32)
        attend_pairs(queries, rows, keys, values, near, bias, mixed, rows)
        return carry

    inner = WIN // QB
    lax.fori_loop(inner, inner + 1, self_rows, 0)

    part_swap.wait()
    joined[pl.ds(before, patch_dev), :] = (part_mine[...] + part_peer[...]).astype(BF16)

    @pl.when(has_right)
    def _():
        rep_right.start()
        halo_send.wait_send()

    @pl.when(has_left)
    def _():
        rep_left.start()
        halo_send.wait_recv()
        halo_swap.start()

    lax.fori_loop(inner + 1, seg // QB, self_rows, 0)

    @pl.when(has_right)
    def _():
        rep_right.wait_send()
        rep_left.wait_recv()
        back_swap.start()

    @pl.when(has_left)
    def _():
        rep_left.wait_send()
        rep_right.wait_recv()
        front_swap.start()
        halo_swap.wait()

    @pl.when(jnp.logical_not(has_left))
    def _():
        halo[...] = jnp.zeros_like(halo)
        joined[front, :] = jnp.zeros((before, width), BF16)

    @pl.when(jnp.logical_not(has_right))
    def _():
        joined[back, :] = jnp.zeros((after, width), BF16)

    hidden = norm_rows(halo[...], gain[...][None, :])
    keys[:WIN, :] = mm(hidden, wk[...]).astype(BF16)
    values[:WIN, :] = mm(hidden, wv[...]).astype(BF16)
    lax.fori_loop(0, inner, self_rows, 0)

    @pl.when(has_right)
    def _():
        back_swap.wait()

    @pl.when(has_left)
    def _():
        front_swap.wait()

    for load in loads[7:]:
        load.wait()
    used = joined.shape[0]
    for weight, target in ((ck, patch_keys), (cv, patch_values)):
        target[:used, :] = mm(joined[...], weight[...]).astype(BF16)
        target[used:, :] = jnp.zeros((target.shape[0] - used, cols), BF16)

    slots = patch_keys.shape[0] - LANES
    slot_row = lax.broadcasted_iota(jnp.int32, (QB, slots), 0)

    def out_swap(step):
        rows = pl.ds(pl.multiple_of(step * QB, QB), QB)
        return send(far.at[rows, :], far_peer.at[rows, :], 8 + step, peer)

    def finish(step):
        out_swap(step).wait()
        rows = pl.ds(pl.multiple_of(step * QB, QB), QB)
        out[rows, :] = (own[rows, :] + far_peer[rows, :].astype(F32)).astype(BF16)

    def cross_block(step, carry):
        rows = pl.ds(pl.multiple_of(step * QB, QB), QB)
        base = pl.multiple_of(lax.rem(lax.div(step, inner), 2) * LANES, LANES)
        near = pl.ds(base, slots)
        first = starts[:1, near]
        allowed = (first <= slot_row + step * QB) & (first >= low_key[rows, :1])
        bias = jnp.where(allowed, 0.0, FAR).astype(F32)
        attend_pairs(cross_rows, rows, patch_keys, patch_values, near, bias, cross, slice(None))
        far[rows, :] = (mm(mixed[rows, :], so[:, there]) + mm(cross[...], co[:, there])).astype(BF16)
        out_swap(step).start()
        own[rows, :] = mm(mixed[rows, :], so[:, here]) + mm(cross[...], co[:, here])

        @pl.when(step > 0)
        def _():
            finish(step - 1)

        return carry

    lax.fori_loop(0, seg // QB, cross_block, 0)
    finish(seg // QB - 1)


def write_kernel(source, target, sem):
    copy = pltpu.make_async_copy(source, target, sem)
    copy.start()
    copy.wait()


def pair_device(
    latent, latent_gain, proj_weight, patch_starts, stream, doc_starts, stream_gain,
    self_query, self_key, self_value, self_out, cross_query, cross_key, cross_value, cross_out,
):
    seg, width = stream.shape
    patch_dev, features = latent.shape
    cols = self_query.shape[1]
    before, after = WIN * patch_dev // seg + DRIFT, DRIFT
    used = before + patch_dev + after
    slots = (used + LANES - 1) // LANES * LANES

    big = (latent, proj_weight, stream, self_key, self_value, self_query, cross_query, cross_key, cross_value, self_out, cross_out)
    small = (latent_gain, stream_gain, patch_starts[None, :], doc_starts[None, :])
    blocks = seg // QB
    update = pl.pallas_call(
        layer_kernel,
        in_specs=[pl.BlockSpec(memory_space=pl.ANY)] * len(big)
        + [pl.BlockSpec(memory_space=pltpu.VMEM)] * len(small),
        out_specs=pl.BlockSpec(memory_space=pltpu.VMEM),
        out_shape=jax.ShapeDtypeStruct((seg, cols), BF16),
        scratch_shapes=[pltpu.VMEM(array.shape, BF16) for array in big]
        + [
            pltpu.VMEM((WIN, width), BF16),
            pltpu.VMEM((WIN + seg, cols), BF16),
            pltpu.VMEM((WIN + seg, cols), BF16),
            pltpu.VMEM((seg, cols), BF16),
            pltpu.VMEM((seg, cols), BF16),
            pltpu.VMEM((seg, cols), BF16),
            pltpu.VMEM((QB, cols), BF16),
            pltpu.VMEM((patch_dev, LANES), F32),
            pltpu.VMEM((patch_dev, LANES), F32),
            pltpu.VMEM((patch_dev, width), F32),
            pltpu.VMEM((patch_dev, width), F32),
            pltpu.VMEM((used, width), BF16),
            pltpu.VMEM((slots, cols), BF16),
            pltpu.VMEM((slots, cols), BF16),
            pltpu.VMEM((seg, cols), F32),
            pltpu.VMEM((seg, cols), BF16),
            pltpu.VMEM((seg, cols), BF16),
            pltpu.VMEM((8, slots), jnp.int32),
            pltpu.VMEM((seg, LANES), jnp.int32),
            pltpu.SemaphoreType.DMA((len(big),)),
            pltpu.SemaphoreType.DMA((8 + blocks,)),
            pltpu.SemaphoreType.DMA((8 + blocks,)),
        ],
        compiler_params=pltpu.CompilerParams(
            collective_id=0, has_side_effects=True, vmem_limit_bytes=60 << 20
        ),
    )(*big, *small)
    return pl.pallas_call(
        write_kernel,
        in_specs=[pl.BlockSpec(memory_space=pltpu.VMEM)],
        out_specs=pl.BlockSpec(memory_space=pl.ANY),
        out_shape=jax.ShapeDtypeStruct((seg, cols), BF16),
        scratch_shapes=[pltpu.SemaphoreType.DMA],
    )(update)


def solution(mesh):
    in_specs = (
        P("seq", "tp"), P("tp"), P("tp", None), P(), P("seq", None), P("seq"), P(),
        P(None, "tp"), P(None, "tp"), P(None, "tp"), P("tp", None),
        P(None, "tp"), P(None, "tp"), P(None, "tp"), P("tp", None),
    )
    return jax.shard_map(
        pair_device if mesh.shape["tp"] == 2 else general_device, mesh=mesh, in_specs=in_specs, out_specs=P("seq", "tp"), check_vma=False
    )
```

```python
import jax
import jax.numpy as jnp
from jax import lax
from jax.experimental import pallas as pl
from jax.experimental.pallas import tpu as pltpu
from jax.sharding import PartitionSpec as P

HD = 64
WIN = 512
PMAX = 448
DRIFT = 32
LANES = 128
QB = 256
F32 = jnp.float32
BF16 = jnp.bfloat16
FAR = -1e30
MESH = pl.DeviceIdType.MESH


def norm_rows(values, gain):
    widened = values.astype(F32)
    mean_square = jnp.mean(widened * widened, axis=1, keepdims=True)
    return (widened * lax.rsqrt(mean_square + 1e-05) * gain.astype(F32)).astype(BF16)


def mm(left, right):
    return jnp.dot(left, right, preferred_element_type=F32)


def score_pair(query, keys):
    low = lax.broadcasted_iota(jnp.int32, query.shape, 1) < HD
    zero = jnp.zeros_like(query)
    scaled = query * jnp.asarray(HD**-0.5, BF16)
    both = jnp.concatenate([jnp.where(low, scaled, zero), jnp.where(low, zero, scaled)], axis=0)
    return lax.dot_general(both, keys, (((1,), (1,)), ((), ())), preferred_element_type=F32)


def mix_pair(scores, values, bias):
    rows = bias.shape[0]
    wide = jnp.concatenate([values, jnp.ones_like(values)], axis=1)
    totals = []
    for part in range(2):
        one = scores[part * rows : (part + 1) * rows] + bias
        top = jnp.max(one, axis=1, keepdims=True)
        totals.append(mm(jnp.exp(one - top).astype(BF16), wide))
    low = lax.broadcasted_iota(jnp.int32, (rows, LANES), 1) < HD
    upper = jnp.where(low, totals[0][:, :LANES], totals[1][:, :LANES])
    lower = jnp.where(low, totals[0][:, LANES:], totals[1][:, LANES:])
    return (upper / lower).astype(BF16)


def attend_pairs(query, rows, keys, values, near, bias, out, out_rows):
    places = [slice(col, col + LANES) for col in range(0, query.shape[1], LANES)]
    scores = score_pair(query[rows, places[0]], keys[near, places[0]])
    for number, at in enumerate(places):
        ready = scores
        if number + 1 < len(places):
            ahead = places[number + 1]
            scores = score_pair(query[rows, ahead], keys[near, ahead])
        out[out_rows, at] = mix_pair(ready, values[near, at], bias)


def from_behind(array, axis, by):
    devices = lax.axis_size(axis)
    pairs = [(i, i + by) for i in range(devices) if 0 <= i + by < devices]
    return lax.ppermute(array, axis, pairs)


def project(left, right):
    return jnp.dot(left, right, preferred_element_type=jnp.float32).astype(jnp.bfloat16)


def attend(query, all_keys, all_values, allowed, head_size):
    row_count = query.shape[0]
    key_count = all_keys.shape[0]
    head_count = query.shape[1] // head_size
    query_heads = query.reshape(row_count, head_count, head_size)
    key_heads = all_keys.reshape(key_count, head_count, head_size)
    value_heads = all_values.reshape(key_count, head_count, head_size)
    scores = jnp.einsum(
        "rhd,khd->hrk", query_heads, key_heads, preferred_element_type=jnp.float32
    ) * head_size ** (-0.5)
    scores = jnp.where(allowed[None], scores, -1e30)
    row_max = jnp.max(scores, axis=2, keepdims=True)
    weights = jnp.where(allowed[None], jnp.exp(scores - row_max), 0.0)
    row_total = jnp.sum(weights, axis=2, keepdims=True)
    probs = (weights / row_total).astype(jnp.bfloat16)
    head_mix = jnp.einsum("hrk,khd->rhd", probs, value_heads, preferred_element_type=jnp.float32)
    return head_mix.reshape(row_count, head_count * head_size).astype(jnp.bfloat16)


def general_device(
    latent,
    latent_gain,
    proj_weight,
    patch_starts,
    stream,
    doc_starts,
    stream_gain,
    self_query,
    self_key,
    self_value,
    self_out,
    cross_query,
    cross_key,
    cross_value,
    cross_out,
):
    seg_bytes = stream.shape[0]
    patch_dev = latent.shape[0]
    slot_count = PMAX
    seq_place = lax.axis_index("seq")
    first_byte = seq_place * seg_bytes
    total_bytes = seg_bytes * lax.axis_size("seq")
    head_size = HD
    widened = latent.astype(jnp.float32)
    square_sum = lax.psum(jnp.sum(widened * widened, axis=1), "tp")
    full_width = latent.shape[1] * lax.axis_size("tp")
    latent_normed = (
        widened
        * lax.rsqrt(square_sum / full_width + 1e-05)[:, None]
        * latent_gain.astype(jnp.float32)
    ).astype(jnp.bfloat16)
    partial_value = jnp.dot(latent_normed, proj_weight, preferred_element_type=jnp.float32)
    offset = jnp.sum((patch_starts < first_byte - WIN).astype(jnp.int32))
    anchor = offset - (seq_place - 1) * patch_dev
    rep_share = lax.psum_scatter(partial_value, "tp", scatter_dimension=1, tiled=True).astype(
        jnp.bfloat16
    )
    arrived = [from_behind(rep_share, "seq", towards) for towards in (1, -1)]
    joined = jnp.concatenate([arrived[0], rep_share, arrived[1]], axis=0)
    own_rows = lax.dynamic_slice_in_dim(joined, anchor, slot_count, 0)
    block_piece = lax.all_gather(own_rows, "tp", axis=1, tiled=True)
    key_total = jnp.dot(block_piece, cross_key, preferred_element_type=jnp.float32)
    value_total = jnp.dot(block_piece, cross_value, preferred_element_type=jnp.float32)
    patch_keys = key_total.astype(jnp.bfloat16)
    patch_values = value_total.astype(jnp.bfloat16)
    hidden = norm_rows(stream, stream_gain)
    own_query = project(hidden, self_query)
    own_key = project(hidden, self_key)
    own_value = project(hidden, self_value)
    cross_rows = project(hidden, cross_query)
    tail_rows = jnp.stack([own_key[seg_bytes - WIN :], own_value[seg_bytes - WIN :]])
    halo_rows = from_behind(tail_rows, "seq", 1)
    near_keys = jnp.concatenate([halo_rows[0], own_key], axis=0)
    near_values = jnp.concatenate([halo_rows[1], own_value], axis=0)
    positions = first_byte + jnp.arange(seg_bytes, dtype=jnp.int32)
    key_pos = first_byte - WIN + jnp.arange(WIN + seg_bytes, dtype=jnp.int32)
    allowed = (
        (key_pos[None, :] <= positions[:, None])
        & (key_pos[None, :] >= positions[:, None] - WIN)
        & (key_pos[None, :] >= doc_starts[:, None])
    )
    self_mixed = attend(own_query, near_keys, near_values, allowed, head_size)
    patch_total = patch_starts.shape[0]
    slot_index = offset + jnp.arange(slot_count, dtype=jnp.int32)
    slot_starts = jnp.where(
        slot_index < patch_total,
        jnp.take(patch_starts, jnp.minimum(slot_index, patch_total - 1)),
        total_bytes,
    )
    cross_allowed = (
        (slot_starts[None, :] <= positions[:, None])
        & (slot_starts[None, :] >= doc_starts[:, None])
        & (slot_starts[None, :] >= positions[:, None] - WIN)
    )
    cross_mixed = attend(cross_rows, patch_keys, patch_values, cross_allowed, head_size)
    partial_out = jnp.dot(self_mixed, self_out, preferred_element_type=jnp.float32) + jnp.dot(
        cross_mixed, cross_out, preferred_element_type=jnp.float32
    )
    return lax.psum_scatter(partial_out.astype(jnp.bfloat16), "tp", scatter_dimension=1, tiled=True)


def layer_kernel(
    latent_h, proj_h, stream_h, wk_h, wv_h, wq_h, wc_h, ck_h, cv_h, so_h, co_h,
    latent_gain, gain, patch_starts, doc_starts, out,
    latent, proj, stream, wk, wv, wq, wc, ck, cv, so, co,
    halo, keys, values, queries, cross_rows, mixed, cross, sq_mine, sq_peer, part_mine, part_peer,
    joined, patch_keys, patch_values, own, far, far_peer, starts, low_key, done, done_sem, local_sem, send_sem, recv_sem,
):
    seg, width = stream.shape
    cols = wk.shape[1]
    patch_dev = latent.shape[0]
    place, place_seq = lax.axis_index("tp"), lax.axis_index("seq")
    last = lax.axis_size("seq") - 1
    peer = {"tp": 1 - place}
    right, left = {"seq": jnp.minimum(place_seq + 1, last)}, {"seq": jnp.maximum(place_seq - 1, 0)}
    has_left, has_right = place_seq > 0, place_seq < last
    here = pl.ds(pl.multiple_of(place * cols, cols), cols)
    there = pl.ds(pl.multiple_of((1 - place) * cols, cols), cols)

    pairs = (
        (latent_h, latent), (stream_h, stream), (wk_h, wk), (wv_h, wv), (wq_h, wq), (wc_h, wc),
        (proj_h, proj), (ck_h, ck), (cv_h, cv), (so_h, so), (co_h, co),
    )
    loads = [pltpu.make_async_copy(a, b, local_sem.at[i]) for i, (a, b) in enumerate(pairs)]
    for load in loads[:6]:
        load.start()

    barrier = pltpu.get_barrier_semaphore()
    pl.semaphore_signal(barrier, inc=1, device_id=peer, device_id_type=MESH)

    @pl.when(has_left)
    def _():
        pl.semaphore_signal(barrier, inc=1, device_id=left, device_id_type=MESH)

    @pl.when(has_right)
    def _():
        pl.semaphore_signal(barrier, inc=1, device_id=right, device_id_type=MESH)

    pl.semaphore_wait(barrier, 1 + has_left.astype(jnp.int32) + has_right.astype(jnp.int32))

    def send(source, target, index, to):
        return pltpu.make_async_remote_copy(
            src_ref=source, dst_ref=target, send_sem=send_sem.at[index], recv_sem=recv_sem.at[index],
            device_id=to, device_id_type=MESH,
        )

    half = WIN // 2
    mine = pl.ds(pl.multiple_of(place * half, half), half)
    tail = pl.ds(pl.multiple_of(seg - WIN + place * half, half), half)
    halo_send = send(stream_h.at[tail, :], halo.at[mine, :], 0, right)
    halo_swap = send(halo.at[mine, :], halo.at[mine, :], 1, peer)
    sq_swap = send(sq_mine, sq_peer, 2, peer)
    part_swap = send(part_mine, part_peer, 3, peer)
    after = DRIFT
    before = joined.shape[0] - patch_dev - after
    front, back = pl.ds(0, before), pl.ds(before + patch_dev, after)
    rep_right = send(joined.at[pl.ds(patch_dev, before), here], joined.at[front, here], 4, right)
    rep_left = send(joined.at[pl.ds(before, after), here], joined.at[back, here], 5, left)
    front_swap = send(joined.at[front, here], joined.at[front, here], 6, peer)
    back_swap = send(joined.at[back, here], joined.at[back, here], 7, peer)

    @pl.when(has_right)
    def _():
        halo_send.start()

    first_byte = place_seq * seg
    byte = lax.broadcasted_iota(jnp.int32, (LANES, LANES), 1)
    for at in range(0, seg, LANES):
        lowest = jnp.maximum(byte + (at - WIN), doc_starts[:, at : at + LANES] - first_byte)
        low_key[at : at + LANES, :] = lowest.T
    behind = pl.ds(pl.multiple_of(jnp.maximum(place_seq - 1, 0) * patch_dev, LANES), patch_dev)
    own_patches = pl.ds(pl.multiple_of(place_seq * patch_dev, LANES), patch_dev)
    ahead = pl.ds(pl.multiple_of(jnp.minimum(place_seq + 1, last) * patch_dev, LANES), LANES)
    tight = jnp.concatenate(
        [
            jnp.where(has_left, patch_starts[:, behind] - first_byte, seg),
            patch_starts[:, own_patches] - first_byte,
            jnp.where(has_right, patch_starts[:, ahead] - first_byte, seg),
        ],
        axis=1,
    )
    span = tight.shape[1]
    skipped = patch_dev - before
    tight = pltpu.roll(jnp.broadcast_to(tight, (8, span)), span - skipped, 1)[:, : starts.shape[1]]
    slot = lax.broadcasted_iota(jnp.int32, tight.shape, 1)
    starts[...] = jnp.where(slot < joined.shape[0], tight, seg)

    loads[0].wait()
    widened = latent[...].astype(F32)
    square = jnp.sum(widened * widened, axis=1, keepdims=True)
    sq_mine[...] = jnp.broadcast_to(square, sq_mine.shape)
    sq_swap.start()

    for load in loads[1:6]:
        load.wait()
    for load in loads[6:]:
        load.start()

    def project_rows(step, carry):
        rows = pl.ds(pl.multiple_of(step * QB, QB), QB)
        shifted = pl.ds(pl.multiple_of(step * QB + WIN, QB), QB)
        hidden = norm_rows(stream[rows, :], gain[...][None, :])
        keys[shifted, :] = mm(hidden, wk[...]).astype(BF16)
        values[shifted, :] = mm(hidden, wv[...]).astype(BF16)
        queries[rows, :] = mm(hidden, wq[...]).astype(BF16)
        cross_rows[rows, :] = mm(hidden, wc[...]).astype(BF16)
        return carry

    lax.fori_loop(0, seg // QB, project_rows, 0)

    loads[6].wait()
    sq_swap.wait()
    scale = lax.rsqrt((sq_mine[:, :1] + sq_peer[:, :1]) / (2 * latent.shape[1]) + 1e-05)
    normed = (latent[...].astype(F32) * scale * latent_gain[...][None, :].astype(F32)).astype(BF16)
    part_mine[...] = mm(normed, proj[...])
    part_swap.start()

    count = WIN + QB
    index = lax.broadcasted_iota(jnp.int32, (QB, count), 1)
    row = lax.broadcasted_iota(jnp.int32, (QB, count), 0)

    def self_rows(step, carry):
        base = pl.multiple_of(step * QB, QB)
        rows, near = pl.ds(base, QB), pl.ds(base, count)
        allowed = (index <= row + WIN) & (index >= low_key[rows, :1] + (WIN - base))
        bias = jnp.where(allowed, 0.0, FAR).astype(F32)
        attend_pairs(queries, rows, keys, values, near, bias, mixed, rows)
        return carry

    inner = WIN // QB
    lax.fori_loop(inner, inner + 1, self_rows, 0)

    part_swap.wait()
    joined[pl.ds(before, patch_dev), :] = (part_mine[...] + part_peer[...]).astype(BF16)

    @pl.when(has_right)
    def _():
        rep_right.start()
        halo_send.wait_send()

    @pl.when(has_left)
    def _():
        rep_left.start()
        halo_send.wait_recv()
        halo_swap.start()

    lax.fori_loop(inner + 1, seg // QB, self_rows, 0)

    @pl.when(has_right)
    def _():
        rep_right.wait_send()
        rep_left.wait_recv()
        back_swap.start()

    @pl.when(has_left)
    def _():
        rep_left.wait_send()
        rep_right.wait_recv()
        front_swap.start()
        halo_swap.wait()

    @pl.when(jnp.logical_not(has_left))
    def _():
        halo[...] = jnp.zeros_like(halo)
        joined[front, :] = jnp.zeros((before, width), BF16)

    @pl.when(jnp.logical_not(has_right))
    def _():
        joined[back, :] = jnp.zeros((after, width), BF16)

    hidden = norm_rows(halo[...], gain[...][None, :])
    keys[:WIN, :] = mm(hidden, wk[...]).astype(BF16)
    values[:WIN, :] = mm(hidden, wv[...]).astype(BF16)
    lax.fori_loop(0, inner, self_rows, 0)

    @pl.when(has_right)
    def _():
        back_swap.wait()

    @pl.when(has_left)
    def _():
        front_swap.wait()

    for load in loads[7:]:
        load.wait()
    used = joined.shape[0]
    for weight, target in ((ck, patch_keys), (cv, patch_values)):
        target[:used, :] = mm(joined[...], weight[...]).astype(BF16)
        target[used:, :] = jnp.zeros((target.shape[0] - used, cols), BF16)

    slots = patch_keys.shape[0] - LANES
    slot_row = lax.broadcasted_iota(jnp.int32, (QB, slots), 0)

    def out_swap(step):
        rows = pl.ds(pl.multiple_of(step * QB, QB), QB)
        return send(far.at[rows, :], far_peer.at[rows, :], 8 + step, peer)

    def write_out(step):
        rows = pl.ds(pl.multiple_of(step * QB, QB), QB)
        return pltpu.make_async_copy(done.at[rows, :], out.at[rows, :], done_sem.at[step])

    def finish(step):
        out_swap(step).wait()
        rows = pl.ds(pl.multiple_of(step * QB, QB), QB)
        done[rows, :] = (own[rows, :] + far_peer[rows, :].astype(F32)).astype(BF16)
        write_out(step).start()

    def cross_block(step, carry):
        rows = pl.ds(pl.multiple_of(step * QB, QB), QB)
        base = pl.multiple_of(lax.rem(lax.div(step, inner), 2) * LANES, LANES)
        near = pl.ds(base, slots)
        first = starts[:1, near]
        allowed = (first <= slot_row + step * QB) & (first >= low_key[rows, :1])
        bias = jnp.where(allowed, 0.0, FAR).astype(F32)
        attend_pairs(cross_rows, rows, patch_keys, patch_values, near, bias, cross, slice(None))
        far[rows, :] = (mm(mixed[rows, :], so[:, there]) + mm(cross[...], co[:, there])).astype(BF16)
        out_swap(step).start()
        own[rows, :] = mm(mixed[rows, :], so[:, here]) + mm(cross[...], co[:, here])

        @pl.when(step > 0)
        def _():
            finish(step - 1)

        return carry

    lax.fori_loop(0, seg // QB, cross_block, 0)
    finish(seg // QB - 1)
    for step in range(seg // QB):
        write_out(step).wait()


def write_kernel(source, target, held, in_sem, out_sem):
    blocks = in_sem.shape[0]
    size = source.shape[0] // blocks
    rows = [pl.ds(block * size, size) for block in range(blocks)]
    takes = [pltpu.make_async_copy(source.at[r, :], held.at[r, :], in_sem.at[i]) for i, r in enumerate(rows)]
    gives = [pltpu.make_async_copy(held.at[r, :], target.at[r, :], out_sem.at[i]) for i, r in enumerate(rows)]
    for take in takes:
        take.start()
    for take, give in zip(takes, gives):
        take.wait()
        give.start()
    for give in gives:
        give.wait()


def pair_device(
    latent, latent_gain, proj_weight, patch_starts, stream, doc_starts, stream_gain,
    self_query, self_key, self_value, self_out, cross_query, cross_key, cross_value, cross_out,
):
    seg, width = stream.shape
    patch_dev, features = latent.shape
    cols = self_query.shape[1]
    before, after = WIN * patch_dev // seg + DRIFT, DRIFT
    used = before + patch_dev + after
    slots = (used + LANES - 1) // LANES * LANES

    big = (latent, proj_weight, stream, self_key, self_value, self_query, cross_query, cross_key, cross_value, self_out, cross_out)
    small = (latent_gain, stream_gain, patch_starts[None, :], doc_starts[None, :])
    blocks = seg // QB
    update = pl.pallas_call(
        layer_kernel,
        in_specs=[pl.BlockSpec(memory_space=pl.ANY)] * len(big)
        + [pl.BlockSpec(memory_space=pltpu.VMEM)] * len(small),
        out_specs=pl.BlockSpec(memory_space=pl.ANY),
        out_shape=jax.ShapeDtypeStruct((seg, cols), BF16),
        scratch_shapes=[pltpu.VMEM(array.shape, BF16) for array in big]
        + [
            pltpu.VMEM((WIN, width), BF16),
            pltpu.VMEM((WIN + seg, cols), BF16),
            pltpu.VMEM((WIN + seg, cols), BF16),
            pltpu.VMEM((seg, cols), BF16),
            pltpu.VMEM((seg, cols), BF16),
            pltpu.VMEM((seg, cols), BF16),
            pltpu.VMEM((QB, cols), BF16),
            pltpu.VMEM((patch_dev, LANES), F32),
            pltpu.VMEM((patch_dev, LANES), F32),
            pltpu.VMEM((patch_dev, width), F32),
            pltpu.VMEM((patch_dev, width), F32),
            pltpu.VMEM((used, width), BF16),
            pltpu.VMEM((slots, cols), BF16),
            pltpu.VMEM((slots, cols), BF16),
            pltpu.VMEM((seg, cols), F32),
            pltpu.VMEM((seg, cols), BF16),
            pltpu.VMEM((seg, cols), BF16),
            pltpu.VMEM((8, slots), jnp.int32),
            pltpu.VMEM((seg, LANES), jnp.int32),
            pltpu.VMEM((seg, cols), BF16),
            pltpu.SemaphoreType.DMA((blocks,)),
            pltpu.SemaphoreType.DMA((len(big),)),
            pltpu.SemaphoreType.DMA((8 + blocks,)),
            pltpu.SemaphoreType.DMA((8 + blocks,)),
        ],
        compiler_params=pltpu.CompilerParams(
            collective_id=0, has_side_effects=True, vmem_limit_bytes=60 << 20
        ),
    )(*big, *small)
    return pl.pallas_call(
        write_kernel,
        in_specs=[pl.BlockSpec(memory_space=pl.ANY)],
        out_specs=pl.BlockSpec(memory_space=pl.ANY),
        out_shape=jax.ShapeDtypeStruct((seg, cols), BF16),
        scratch_shapes=[
            pltpu.VMEM((seg, cols), BF16),
            pltpu.SemaphoreType.DMA((2 * blocks,)),
            pltpu.SemaphoreType.DMA((2 * blocks,)),
        ],
    )(update)


def solution(mesh):
    in_specs = (
        P("seq", "tp"), P("tp"), P("tp", None), P(), P("seq", None), P("seq"), P(),
        P(None, "tp"), P(None, "tp"), P(None, "tp"), P("tp", None),
        P(None, "tp"), P(None, "tp"), P(None, "tp"), P("tp", None),
    )
    return jax.shard_map(
        pair_device if mesh.shape["tp"] == 2 else general_device, mesh=mesh, in_specs=in_specs, out_specs=P("seq", "tp"), check_vma=False
    )
```
